32 devices in a mesh: gx: 8 (over y, x, core), gy: 4 (over z).
Axes of the slice: x: 2, y: 2, z: 4, core: 2. Of those that a mesh axis runs over, the one named last changes fastest.
Arguments:
- u_now_c: float32 [3, 16, 16, 128], P(None, 'gx', 'gy'), may hold values from -6 to 6
- u_prev_c: float32 [3, 16, 16, 128], P(None, 'gx', 'gy'), may hold values from -6 to 6
- memory_c: float32 [3, 3, 16, 16, 128], P(None, None, 'gx', 'gy'), may hold values from -3 to 3
- mu_c: float32 [16, 16, 128], P('gx', 'gy'), may hold values from 0.5 to 1.5
- lam_c: float32 [16, 16, 128], P('gx', 'gy'), may hold values from 0.5 to 1.5
- rho_c: float32 [16, 16, 128], P('gx', 'gy'), may hold values from 1 to 2
- q_c: float32 [3, 16, 16, 128], P(None, 'gx', 'gy'), may hold values from 0.05 to 0.4
- omega_c: float32 [3, 16, 16, 128], P(None, 'gx', 'gy'), may hold values from 0.1 to 8
- u_now_f: float32 [3, 32, 32, 128], P(None, 'gx', 'gy'), may hold values from -6 to 6
- u_prev_f: float32 [3, 32, 32, 128], P(None, 'gx', 'gy'), may hold values from -6 to 6
- memory_f: float32 [3, 3, 32, 32, 128], P(None, None, 'gx', 'gy'), may hold values from -3 to 3
- mu_f: float32 [32, 32, 128], P('gx', 'gy'), may hold values from 0.5 to 1.5
- lam_f: float32 [32, 32, 128], P('gx', 'gy'), may hold values from 0.5 to 1.5
- rho_f: float32 [32, 32, 128], P('gx', 'gy'), may hold values from 1 to 2
- q_f: float32 [3, 32, 32, 128], P(None, 'gx', 'gy'), may hold values from 0.05 to 0.4
- omega_f: float32 [3, 32, 32, 128], P(None, 'gx', 'gy'), may hold values from 0.1 to 8
- stretch_f: float32 [32, 32], P('gx', 'gy'), may hold values from 0.35 to 0.7
Outputs:
- u_out_c: float32 [3, 16, 16, 128], P(None, 'gx', 'gy')
- u_out_f: float32 [3, 32, 32, 128], P(None, 'gx', 'gy')
- memory_out_c: float32 [3, 3, 16, 16, 128], P(None, None, 'gx', 'gy')
- memory_out_f: float32 [3, 3, 32, 32, 128], P(None, None, 'gx', 'gy')
The draws below stay inside these ranges and needn't reach their ends.
All inputs are finite; a program needn't handle non-finite values.
Results may differ from the reference program's by a relative error of at most 0.0001.
Values sent between devices are 32-bit elements; how exact they have to be, the bound alone decides.
A program may use at most 64 MiB of HBM per device.

```python
import math
import jax
import jax.numpy as jnp

NZC = 128
NZF = 128
STEPS = 2
NX = 16
NY = 16
FX = 32
FY = 32


def level_of(rng, dims, shards, smallest, largest):
    factor_of = 1.0
    for position, shards_of in shards:
        draws = jax.random.uniform(jax.random.fold_in(jax.random.fold_in(rng, 6), position), (shards_of,), jnp.float32, smallest / len(shards), largest / len(shards))
        factor_of = factor_of * jnp.repeat(jnp.exp(draws), dims[position] // shards_of).reshape((-1,) + (1,) * (len(dims) - 1 - position))
    return factor_of


def scatter_about(own_key, dims, deviation, bound, split=(), dtype=jnp.bfloat16):
    gain = level_of(own_key, dims, split, -0.22, 0.18) if split else 1.0
    array = jax.random.normal(own_key, dims, jnp.float32) * deviation * gain
    return jnp.minimum(jnp.maximum(array, -bound), bound).astype(dtype)


def setup_inputs(seed: int = 0) -> dict:
    seeds = jax.random.split(jax.random.key(seed), 18)
    return {
        "u_now_c": scatter_about(seeds[0], (3, NX, NY, NZC), 1.0, 6.0, ((1, 8), (2, 4)), jnp.float32),
        "u_prev_c": scatter_about(seeds[1], (3, NX, NY, NZC), 1.0, 6.0, ((1, 8), (2, 4)), jnp.float32),
        "memory_c": scatter_about(seeds[2], (3, 3, NX, NY, NZC), 0.5, 3.0, ((2, 8), (3, 4)), jnp.float32),
        "mu_c": jnp.clip(0.5 + 1.0 * jax.random.uniform(seeds[3], (NX, NY, NZC), jnp.float32) ** level_of(seeds[3], (NX, NY, NZC), ((0, 8), (1, 4)), -0.2, 0.2), 0.5, 1.5),
        "lam_c": jnp.clip(0.5 + 1.0 * jax.random.uniform(seeds[4], (NX, NY, NZC), jnp.float32) ** level_of(seeds[4], (NX, NY, NZC), ((0, 8), (1, 4)), -0.2, 0.2), 0.5, 1.5),
        "rho_c": jnp.clip(1.0 + 1.0 * jax.random.uniform(seeds[5], (NX, NY, NZC), jnp.float32) ** level_of(seeds[5], (NX, NY, NZC), ((0, 8), (1, 4)), -0.2, 0.2), 1.0, 2.0),
        "q_c": jnp.clip(jnp.exp(math.log(0.4) - 2.0794415 * jax.random.uniform(seeds[6], (3, NX, NY, NZC), jnp.float32) ** level_of(seeds[6], (3, NX, NY, NZC), ((1, 8), (2, 4)), -0.2, 0.2)), 0.05, 0.4),
        "omega_c": jnp.clip(jnp.exp(math.log(8.0) - 4.3820266 * jax.random.uniform(seeds[7], (3, NX, NY, NZC), jnp.float32) ** level_of(seeds[7], (3, NX, NY, NZC), ((1, 8), (2, 4)), -0.2, 0.2)), 0.1, 8.0),
        "u_now_f": scatter_about(seeds[8], (3, FX, FY, NZF), 1.0, 6.0, ((1, 8), (2, 4)), jnp.float32),
        "u_prev_f": scatter_about(seeds[9], (3, FX, FY, NZF), 1.0, 6.0, ((1, 8), (2, 4)), jnp.float32),
        "memory_f": scatter_about(seeds[10], (3, 3, FX, FY, NZF), 0.5, 3.0, ((2, 8), (3, 4)), jnp.float32),
        "mu_f": jnp.clip(0.5 + 1.0 * jax.random.uniform(seeds[11], (FX, FY, NZF), jnp.float32) ** level_of(seeds[11], (FX, FY, NZF), ((0, 8), (1, 4)), -0.2, 0.2), 0.5, 1.5),
        "lam_f": jnp.clip(0.5 + 1.0 * jax.random.uniform(seeds[12], (FX, FY, NZF), jnp.float32) ** level_of(seeds[12], (FX, FY, NZF), ((0, 8), (1, 4)), -0.2, 0.2), 0.5, 1.5),
        "rho_f": jnp.clip(1.0 + 1.0 * jax.random.uniform(seeds[13], (FX, FY, NZF), jnp.float32) ** level_of(seeds[13], (FX, FY, NZF), ((0, 8), (1, 4)), -0.2, 0.2), 1.0, 2.0),
        "q_f": jnp.clip(jnp.exp(math.log(0.4) - 2.0794415 * jax.random.uniform(seeds[14], (3, FX, FY, NZF), jnp.float32) ** level_of(seeds[14], (3, FX, FY, NZF), ((1, 8), (2, 4)), -0.2, 0.2)), 0.05, 0.4),
        "omega_f": jnp.clip(jnp.exp(math.log(8.0) - 4.3820266 * jax.random.uniform(seeds[15], (3, FX, FY, NZF), jnp.float32) ** level_of(seeds[15], (3, FX, FY, NZF), ((1, 8), (2, 4)), -0.2, 0.2)), 0.1, 8.0),
        "stretch_f": jnp.clip(0.35 + 0.35 * jax.random.uniform(seeds[16], (FX, FY), jnp.float32) ** level_of(seeds[16], (FX, FY), ((0, 8), (1, 4)), -0.2, 0.2), 0.35, 0.7),
    }


DT = 0.1


def restrict(plane):
    comps, wide, tall = plane.shape
    return plane.reshape(comps, wide // 2, 2, tall // 2, 2).mean(axis=(2, 4))


def prolong(plane):
    comps = plane.shape[0]
    even = 0.75 * plane[:, 1:-1] + 0.25 * plane[:, :-2]
    odd = 0.75 * plane[:, 1:-1] + 0.25 * plane[:, 2:]
    rows = jnp.stack([even, odd], axis=2).reshape(comps, -1, plane.shape[2])
    even = 0.75 * rows[:, :, 1:-1] + 0.25 * rows[:, :, :-2]
    odd = 0.75 * rows[:, :, 1:-1] + 0.25 * rows[:, :, 2:]
    return jnp.stack([even, odd], axis=3).reshape(comps, rows.shape[1], -1)


def coarse_extend(field_c, fine_plane):
    top = restrict(fine_plane)[..., None]
    return jnp.concatenate([top, field_c, jnp.zeros_like(top)], axis=3)


def fine_extend(field_f, coarse_padded):
    bottom = prolong(coarse_padded[..., 1])[..., None]
    return jnp.concatenate([field_f[..., :1], field_f, bottom], axis=3)


def shifted(padded, offx, offy, offz):
    sizes = padded.shape
    return padded[:, 1 + offx:sizes[1] - 1 + offx, 1 + offy:sizes[2] - 1 + offy, 1 + offz:sizes[3] - 1 + offz]


def mixed(padded, comp, first, second):
    plus_plus = [0, 0, 0]
    plus_plus[first] = 1
    plus_plus[second] = 1
    plus_minus = [0, 0, 0]
    plus_minus[first] = 1
    plus_minus[second] = -1
    minus_plus = [0, 0, 0]
    minus_plus[first] = -1
    minus_plus[second] = 1
    minus_minus = [0, 0, 0]
    minus_minus[first] = -1
    minus_minus[second] = -1
    total = shifted(padded[comp:comp + 1], *plus_plus) - shifted(padded[comp:comp + 1], *plus_minus)
    total = total - shifted(padded[comp:comp + 1], *minus_plus) + shifted(padded[comp:comp + 1], *minus_minus)
    return total[0]


def operator(padded, shear, lame, level_h, level_hz):
    across = level_h * level_h
    vertical = level_hz * level_hz
    center = shifted(padded, 0, 0, 0)
    dxx = (shifted(padded, 1, 0, 0) + shifted(padded, -1, 0, 0) - 2.0 * center) / across
    dyy = (shifted(padded, 0, 1, 0) + shifted(padded, 0, -1, 0) - 2.0 * center) / across
    dzz = (shifted(padded, 0, 0, 1) + shifted(padded, 0, 0, -1) - 2.0 * center) / vertical
    flat = 4.0 * across
    slant = 4.0 * level_h * level_hz
    grad_x = dxx[0] + mixed(padded, 1, 0, 1) / flat + mixed(padded, 2, 0, 2) / slant
    grad_y = mixed(padded, 0, 0, 1) / flat + dyy[1] + mixed(padded, 2, 1, 2) / slant
    grad_z = mixed(padded, 0, 0, 2) / slant + mixed(padded, 1, 1, 2) / slant + dzz[2]
    return shear * (dxx + dyy + dzz) + (lame + shear) * jnp.stack([grad_x, grad_y, grad_z])


def level_force(full, shear, lame, level_h, level_hz):
    force = operator(full[:3], shear, lame, level_h, level_hz)
    for mech in range(3):
        force = force - operator(full[3 + 3 * mech:6 + 3 * mech], shear, lame, level_h, level_hz)
    return force


def pad_sides(field):
    return jnp.pad(field, ((0, 0), (1, 1), (1, 1), (0, 0)))


def reference(u_now_c, u_prev_c, memory_c, mu_c, lam_c, rho_c, q_c, omega_c, u_now_f, u_prev_f, memory_f, mu_f, lam_f, rho_f, q_f, omega_f, stretch_f):
    height_f = stretch_f[:, :, None]
    for step in range(STEPS):
        prod_c = (q_c[:, None] * memory_c).reshape((9,) + u_now_c.shape[1:])
        prod_f = (q_f[:, None] * memory_f).reshape((9,) + u_now_f.shape[1:])
        field_c = jnp.concatenate([u_now_c, prod_c], axis=0)
        field_f = jnp.concatenate([u_now_f, prod_f], axis=0)
        full_c = pad_sides(coarse_extend(field_c, field_f[..., -1]))
        full_f = pad_sides(fine_extend(field_f, full_c))
        force_c = level_force(full_c, mu_c, lam_c, 1.0, 1.0)
        force_f = level_force(full_f, mu_f, lam_f, 0.5, height_f)
        next_c = 2.0 * u_now_c - u_prev_c + (DT * DT / rho_c) * force_c
        next_f = 2.0 * u_now_f - u_prev_f + (DT * DT / rho_f) * force_f
        memory_c = memory_c + DT * omega_c[:, None] * (u_now_c[None] - memory_c)
        memory_f = memory_f + DT * omega_f[:, None] * (u_now_f[None] - memory_f)
        u_prev_c, u_now_c = u_now_c, next_c
        u_prev_f, u_now_f = u_now_f, next_f
    return u_now_c, u_now_f, memory_c, memory_f
```

```python
import functools

import jax
import jax.numpy as jnp
from jax import lax
from jax.experimental import pallas as pl
from jax.experimental.pallas import tpu as pltpu
from jax.sharding import PartitionSpec as P

STEPS = 2
DT = 0.1
MESH = pl.DeviceIdType.MESH
SIDES = (-1, 1)
CORNERS = tuple((dx, dy) for dx in SIDES for dy in SIDES)
F32 = jnp.float32


class Shape:
    def __init__(self, fine, coarse):
        _, self.fx, self.fy, self.nz = fine
        _, self.cx, self.cy, _ = coarse
        self.x_rows = 3 * self.fy + 6 * self.cy
        self.y_rows = 3 * self.fx + 6 * self.cx
        self.d_rows = 6

    def xf(self, c):
        return pl.ds(c * self.fy, self.fy)

    def xc(self, c):
        return pl.ds(3 * self.fy + c * self.cy, self.cy)

    def xt(self, c):
        return pl.ds(3 * self.fy + (3 + c) * self.cy, self.cy)

    def yf(self, c, x):
        return pl.ds(c * self.fx + x, 1)

    def yc(self, c, x):
        return pl.ds(3 * self.fx + c * self.cx + x, 1)

    def yt(self, c, x):
        return pl.ds(3 * self.fx + (3 + c) * self.cx + x, 1)


def iota(shape, axis):
    return lax.broadcasted_iota(jnp.int32, shape, axis)


def below(tile, ghost):
    n = tile.shape[-1]
    return pltpu.roll(jnp.where(iota(tile.shape, 1) == 0, ghost, tile), n - 1, 1)


def above(tile, ghost):
    n = tile.shape[-1]
    return pltpu.roll(jnp.where(iota(tile.shape, 1) == n - 1, ghost, tile), 1, 1)


def above_same(tile):
    return jnp.where(iota(tile.shape, 1) == 0, tile, pltpu.roll(tile, 1, 1))


def y_minus(tile, row):
    return jnp.concatenate([row, tile[:-1]], axis=0)


def y_plus(tile, row):
    return jnp.concatenate([tile[1:], row], axis=0)


def restrict(first, second):
    total = first + second
    rows = total.shape[0] // 2
    out = jnp.zeros((rows, total.shape[1]), F32)
    where = iota(out.shape, 0)
    for j in range(rows):
        pair = total[2 * j : 2 * j + 1] + total[2 * j + 1 : 2 * j + 2]
        out = jnp.where(where == j, pair, out)
    return 0.25 * out


def columns(stretch, x, size):
    row = stretch[x : x + 1, :]
    eye = iota((size, size), 0) == iota((size, size), 1)
    return jnp.sum(jnp.where(eye, row, 0.0), axis=1, keepdims=True)


def prolong_weights(size, nz):
    y = iota((size, nz), 0)
    out = []
    for j in range(-1, size // 2 + 1):
        near = (y == 2 * j) | (y == 2 * j + 1)
        far = (y == 2 * j + 2) | (y == 2 * j - 1)
        out.append(jnp.where(near, 0.75, jnp.where(far, 0.25, 0.0)).astype(F32))
    return out


def level_force(p, lo, hi, dz, sz, dz_lo, dz_hi, mu, lam, h, hz, emit):
    count = len(p[0]) - 2
    dy, sy = {}, {}
    for c in range(3):
        for x in range(count + 2):
            own = 1 <= x <= count
            if c == 2 and not own:
                continue
            plus = y_plus(p[c][x], hi[c][x])
            minus = y_minus(p[c][x], lo[c][x])
            if c < 2:
                dy[c, x] = plus - minus
            if own:
                sy[c, x] = plus + minus
    flat = 1.0 / (4.0 * h * h)
    ih2 = 1.0 / (h * h)
    for x in range(1, count + 1):
        iz = 1.0 / hz(x - 1)
        iz2 = iz * iz
        slant = iz * (0.25 / h)
        dxx = [(p[c][x + 1] + p[c][x - 1] - 2.0 * p[c][x]) * ih2 for c in range(3)]
        dyy = [(sy[c, x] - 2.0 * p[c][x]) * ih2 for c in range(3)]
        dzz = [(sz[c][x - 1] - 2.0 * p[c][x]) * iz2 for c in range(3)]

        def xz(c):
            return dz[c][x + 1] - dz[c][x - 1]

        def xy(c):
            return dy[c, x + 1] - dy[c, x - 1]

        def yz(c):
            return y_plus(dz[c][x], dz_hi[c][x - 1]) - y_minus(dz[c][x], dz_lo[c][x - 1])

        grad = [
            dxx[0] + xy(1) * flat + xz(2) * slant,
            xy(0) * flat + dyy[1] + yz(2) * slant,
            (xz(0) + yz(1)) * slant + dzz[2],
        ]
        shear, both = mu(x - 1), mu(x - 1) + lam(x - 1)
        emit(x - 1, [shear * (dxx[c] + dyy[c] + dzz[c]) + both * grad[c] for c in range(3)])


def forces(s, inside, nf, nc, tg, rx, ry, rd, mu_f, lam_f, stretch, mu_c, lam_c, emit_f, emit_c):
    nz = s.nz
    pf = [[rx(0)[s.xf(c), :]] + nf[c] + [rx(1)[s.xf(c), :]] for c in range(3)]
    pc = [[rx(0)[s.xc(c), :]] + nc[c] + [rx(1)[s.xc(c), :]] for c in range(3)]
    pt = [[rx(0)[s.xt(c), :]] + tg[c] + [rx(1)[s.xt(c), :]] for c in range(3)]

    def rows(side, c, name, count, base):
        ends = [rd(xs * 2 + side)[pl.ds(base + c, 1), :] for xs in range(2)]
        return [ends[0]] + [ry(side)[name(c, x), :] for x in range(count)] + [ends[1]]

    lo_f, hi_f = ([rows(k, c, s.yf, s.fx, 0) for c in range(3)] for k in range(2))
    lo_c, hi_c = ([rows(k, c, s.yc, s.cx, 3) for c in range(3)] for k in range(2))
    zero_c = jnp.zeros((s.cy, nz), F32)
    zero_r = jnp.zeros((1, nz), F32)

    dz, sz, dz_lo, dz_hi = [], [], [], []
    for c in range(3):
        down = [below(t, zero_c) for t in pc[c]]
        up = [above(t, g) for t, g in zip(pc[c], pt[c])]
        dz.append([d - u for d, u in zip(down, up)])
        sz.append([d + u for d, u in zip(down, up)][1:-1])
        for k, (rows_c, out) in enumerate(((lo_c, dz_lo), (hi_c, dz_hi))):
            out.append(
                [
                    below(rows_c[c][x + 1], zero_r) - above(rows_c[c][x + 1], ry(k)[s.yt(c, x), :])
                    for x in range(s.cx)
                ]
                if c > 0
                else None
            )
    level_force(pc, lo_c, hi_c, dz, sz, dz_lo, dz_hi, mu_c, lam_c, 1.0, lambda x: 1.0, emit_c)

    weights = prolong_weights(s.fy, nz)
    dz, sz, dz_lo, dz_hi = [], [], [], []
    for c in range(3):

        def mixed_x(get, fx):
            i = fx // 2
            other = i - 1 if fx % 2 == 0 else i + 1
            return 0.75 * get(i + 1) + 0.25 * get(other + 1)

        dz_c, sz_c, rows_lo, rows_hi = [], [], [], []
        for fx in range(-1, s.fx + 1):
            own = 0 <= fx < s.fx
            if c == 1 and not own:
                dz_c.append(None)
                continue
            tile = mixed_x(lambda i: pc[c][i], fx)
            low = mixed_x(lambda i: lo_c[c][i], fx)
            high = mixed_x(lambda i: hi_c[c][i], fx)
            parts = [low] + [tile[j : j + 1] for j in range(s.cy)] + [high]
            ghost = sum(w * r for w, r in zip(weights, parts))
            if fx < 0:
                ghost = ghost * inside(-1, 0)
            elif not own:
                ghost = ghost * inside(1, 0)
            t = pf[c][fx + 1]
            down, up = below(t, ghost), above_same(t)
            dz_c.append(down - up)
            if own:
                sz_c.append(down + up)
                if c > 0:
                    g = (0.75 * low + 0.25 * parts[1]) * inside(0, -1)
                    r = lo_f[c][fx + 1]
                    rows_lo.append(below(r, g) - above_same(r))
                    g = (0.75 * high + 0.25 * parts[-2]) * inside(0, 1)
                    r = hi_f[c][fx + 1]
                    rows_hi.append(below(r, g) - above_same(r))
        dz.append(dz_c)
        sz.append(sz_c)
        dz_lo.append(rows_lo)
        dz_hi.append(rows_hi)
    wide = [jnp.broadcast_to(columns(stretch, x, s.fy), (s.fy, nz)) for x in range(s.fx)]
    level_force(pf, lo_f, hi_f, dz, sz, dz_lo, dz_hi, mu_f, lam_f, 0.5, lambda x: wide[x], emit_f)


def top_ghost(s, nf):
    return [[restrict(nf[c][2 * i], nf[c][2 * i + 1]) for i in range(s.cx)] for c in range(3)]


def place(axes):
    gx, gy = axes
    ix, iy = lax.axis_index("gx"), lax.axis_index("gy")

    def exists(dx, dy):
        ok = None
        for here, step, count in ((ix, dx, gx), (iy, dy, gy)):
            if step:
                test = here > 0 if step < 0 else here < count - 1
                ok = test if ok is None else jnp.logical_and(ok, test)
        return ok

    def inside(dx, dy):
        return jnp.where(exists(dx, dy), 1.0, 0.0).astype(F32)

    return ix, iy, exists, inside


def relaxed(memory, omega, u):
    return memory + DT * omega * (u - memory)


def first_kernel(s, axes, *refs):
    levels = {}
    levels["c"] = refs[0:8]
    levels["f"] = refs[8:16]
    stretch_ref = refs[16]
    nf_out, nc_out, tg_out, rx_out, ry_out, rd_out = refs[17:23]
    base_f, base_c, sx, sy, sd, rx, ry, rd, send_sem, recv_sem = refs[23:]
    ix, iy, exists, inside = place(axes)

    one = lambda test: jnp.where(test, 1, 0).astype(jnp.int32)
    along = lambda here, count: one(here > 0) + one(here < count - 1) + 1
    peers = along(ix, axes[0]) * along(iy, axes[1]) - 1
    links = []
    for k, dx in enumerate(SIDES):
        links.append(((dx, 0), sx, rx, k, 1 - k))
    for k, dy in enumerate(SIDES):
        links.append(((0, dy), sy, ry, k, 1 - k))
    for k, (dx, dy) in enumerate(CORNERS):
        links.append(((dx, dy), sd, rd, k, 3 - k))

    barrier = pltpu.get_barrier_semaphore()
    for (dx, dy), *_ in links:

        @pl.when(exists(dx, dy))
        def _():
            pl.semaphore_signal(barrier, inc=1, device_id=(ix + dx, iy + dy), device_id_type=MESH)

    def net_of(level):
        u, _, memory, _, _, _, q, _ = levels[level]
        out = []
        for c in range(3):
            out.append([])
            for x in range(u.shape[1]):
                out[c].append(u[c, x] - sum(q[m, x] * memory[m, c, x] for m in range(3)))
        return out

    def pack(e, nf, nc, tg):
        for k in range(2):
            fx, cx = (0, 0) if k == 0 else (s.fx - 1, s.cx - 1)
            for c in range(3):
                sx[e, k, s.xf(c), :] = nf[c][fx]
                sx[e, k, s.xc(c), :] = nc[c][cx]
                sx[e, k, s.xt(c), :] = tg[c][cx]
            fy, cy = (0, 0) if k == 0 else (s.fy - 1, s.cy - 1)
            for c in range(3):
                for x in range(s.fx):
                    sy[e, k, s.yf(c, x), :] = nf[c][x][fy : fy + 1]
                for x in range(s.cx):
                    sy[e, k, s.yc(c, x), :] = nc[c][x][cy : cy + 1]
                    sy[e, k, s.yt(c, x), :] = tg[c][x][cy : cy + 1]
        for k, (dx, dy) in enumerate(CORNERS):
            fx, cx = (0, 0) if dx < 0 else (s.fx - 1, s.cx - 1)
            fy, cy = (0, 0) if dy < 0 else (s.fy - 1, s.cy - 1)
            for c in range(3):
                sd[e, k, pl.ds(c, 1), :] = nf[c][fx][fy : fy + 1]
                sd[e, k, pl.ds(3 + c, 1), :] = nc[c][cx][cy : cy + 1]

    def copies(e):
        for n, ((dx, dy), src, dst, k, other) in enumerate(links):
            yield (dx, dy), pltpu.make_async_remote_copy(
                src_ref=src.at[e, k],
                dst_ref=dst.at[e, other],
                send_sem=send_sem.at[e, n],
                recv_sem=recv_sem.at[e, 11 - n if n >= 4 else n ^ 1],
                device_id=(ix + dx, iy + dy),
                device_id_type=MESH,
            )

    def start(e):
        for (dx, dy), copy in reversed(list(copies(e))):

            @pl.when(exists(dx, dy))
            def _():
                copy.start()

    def finish(e):
        for (dx, dy), copy in copies(e):

            @pl.when(exists(dx, dy))
            def _():
                copy.wait_send()

        for n, ((dx, dy), src, dst, k, other) in enumerate(links):

            @pl.when(exists(dx, dy))
            def _():
                pltpu.make_async_remote_copy(
                    src_ref=src.at[e, k],
                    dst_ref=dst.at[e, k],
                    send_sem=send_sem.at[e, n],
                    recv_sem=recv_sem.at[e, n],
                    device_id=(ix + dx, iy + dy),
                    device_id_type=MESH,
                ).wait_recv()

    nf, nc = net_of("f"), net_of("c")
    tg = top_ghost(s, nf)
    pack(0, nf, nc, tg)

    pl.semaphore_wait(barrier, peers)

    start(0)

    for (dx, dy), src, dst, k, other in links:

        @pl.when(jnp.logical_not(exists(dx, dy)))
        def _():
            for e in range(2):
                dst[e, k] = jnp.zeros(dst.shape[2:], F32)

    for level, base in (("f", base_f), ("c", base_c)):
        u, prev, memory, _, _, _, q, omega = levels[level]
        for x in range(u.shape[1]):
            for c in range(3):
                here = u[c, x]
                base[c, x] = (
                    2.0 * here
                    - prev[c, x]
                    - sum(q[m, x] * relaxed(memory[m, c, x], omega[m, x], here) for m in range(3))
                )

    finish(0)

    new = {"f": [[None] * s.fx for _ in range(3)], "c": [[None] * s.cx for _ in range(3)]}

    def emit(level, base):
        def put(x, force):
            scale = (DT * DT) / levels[level][5][x]
            for c in range(3):
                new[level][c][x] = base[c, x] + scale * force[c]

        return put

    coef = lambda level, which: (lambda x: levels[level][which][x])
    forces(
        s, inside, nf, nc, tg,
        lambda k: rx.at[0, k], lambda k: ry.at[0, k], lambda k: rd.at[0, k],
        coef("f", 3), coef("f", 4), stretch_ref[...], coef("c", 3), coef("c", 4),
        emit("f", base_f), emit("c", base_c),
    )
    nf, nc = new["f"], new["c"]
    tg = top_ghost(s, nf)
    pack(1, nf, nc, tg)
    start(1)
    for c in range(3):
        for x in range(s.fx):
            nf_out[c, x] = nf[c][x]
        for x in range(s.cx):
            nc_out[c, x] = nc[c][x]
            tg_out[c, x] = tg[c][x]
    finish(1)
    for src, dst in ((rx, rx_out), (ry, ry_out), (rd, rd_out)):
        for k in range(dst.shape[0]):
            dst[k] = src[1, k]


def second_kernel(s, axes, *refs):
    levels = {"c": refs[0:7], "f": refs[7:14]}
    stretch_ref, nf_ref, nc_ref, tg_ref, rx, ry, rd = refs[14:21]
    outs = {"c": (refs[21], refs[23]), "f": (refs[22], refs[24])}
    _, _, _, inside = place(axes)
    nets = {"f": nf_ref, "c": nc_ref}
    tiles = lambda ref: [[ref[c, x] for x in range(ref.shape[1])] for c in range(3)]
    base = {"f": {}, "c": {}}
    for level in ("f", "c"):
        u, memory, _, _, _, q, omega = levels[level]
        for x in range(u.shape[1]):
            for c in range(3):
                here = u[c, x]
                mem = [relaxed(memory[m, c, x], omega[m, x], here) for m in range(3)]
                mid = nets[level][c, x] + sum(q[m, x] * mem[m] for m in range(3))
                for m in range(3):
                    outs[level][1][m, c, x] = relaxed(mem[m], omega[m, x], mid)
                outs[level][0][c, x] = 2.0 * mid - here

    def emit(level):
        def put(x, force):
            scale = (DT * DT) / levels[level][4][x]
            for c in range(3):
                outs[level][0][c, x] = outs[level][0][c, x] + scale * force[c]

        return put

    coef = lambda level, which: (lambda x: levels[level][which][x])
    forces(
        s, inside, tiles(nf_ref), tiles(nc_ref), tiles(tg_ref),
        lambda k: rx.at[k], lambda k: ry.at[k], lambda k: rd.at[k],
        coef("f", 2), coef("f", 3), stretch_ref[...], coef("c", 2), coef("c", 3),
        emit("f"), emit("c"),
    )


def shards(axes, *args):
    c_args, f_args, stretch = args[0:8], args[8:16], args[16]
    s = Shape(f_args[0].shape, c_args[0].shape)
    vmem = pl.BlockSpec(memory_space=pltpu.VMEM)
    sd = lambda *shape: jax.ShapeDtypeStruct(shape, F32)
    mids = pl.pallas_call(
        functools.partial(first_kernel, s, axes),
        out_shape=(
            sd(3, s.fx, s.fy, s.nz),
            sd(3, s.cx, s.cy, s.nz),
            sd(3, s.cx, s.cy, s.nz),
            sd(2, s.x_rows, s.nz),
            sd(2, s.y_rows, s.nz),
            sd(4, s.d_rows, s.nz),
        ),
        in_specs=[vmem] * 17,
        out_specs=[vmem] * 6,
        scratch_shapes=[
            pltpu.VMEM((3, s.fx, s.fy, s.nz), F32),
            pltpu.VMEM((3, s.cx, s.cy, s.nz), F32),
        ]
        + [
            pltpu.VMEM((2, n, rows, s.nz), F32)
            for _ in range(2)
            for n, rows in ((2, s.x_rows), (2, s.y_rows), (4, s.d_rows))
        ]
        + [pltpu.SemaphoreType.DMA((2, 8)), pltpu.SemaphoreType.DMA((2, 8))],
        compiler_params=pltpu.CompilerParams(collective_id=0, has_side_effects=True),
        name="exchange",
    )(*c_args, *f_args, stretch)
    drop = lambda a: a[:1] + a[2:]
    return pl.pallas_call(
        functools.partial(second_kernel, s, axes),
        out_shape=(
            sd(*c_args[0].shape),
            sd(*f_args[0].shape),
            sd(*c_args[2].shape),
            sd(*f_args[2].shape),
        ),
        in_specs=[vmem] * 21,
        out_specs=[vmem] * 4,
        name="finish",
    )(*drop(c_args), *drop(f_args), stretch, *mids)


def solution(mesh):
    axes = (mesh.shape["gx"], mesh.shape["gy"])
    field = P(None, "gx", "gy", None)
    memory = P(None, None, "gx", "gy", None)
    cell = P("gx", "gy", None)
    level = (field, field, memory, cell, cell, cell, field, field)
    return jax.shard_map(
        functools.partial(shards, axes),
        mesh=mesh,
        in_specs=level + level + (P("gx", "gy"),),
        out_specs=(field, field, memory, memory),
        check_vma=False,
    )
```

```python
import functools

import jax
import jax.numpy as jnp
from jax import lax
from jax.experimental import pallas as pl
from jax.experimental.pallas import tpu as pltpu
from jax.sharding import PartitionSpec as P

STEPS = 2
DT = 0.1
MESH = pl.DeviceIdType.MESH
SIDES = (-1, 1)
CORNERS = tuple((dx, dy) for dx in SIDES for dy in SIDES)
F32 = jnp.float32


class Shape:
    def __init__(self, fine, coarse):
        _, self.fx, self.fy, self.nz = fine
        _, self.cx, self.cy, _ = coarse
        self.x_rows = 3 * self.fy + 6 * self.cy
        self.y_rows = 3 * self.fx + 6 * self.cx
        self.d_rows = 6

    def xf(self, c):
        return pl.ds(c * self.fy, self.fy)

    def xc(self, c):
        return pl.ds(3 * self.fy + c * self.cy, self.cy)

    def xt(self, c):
        return pl.ds(3 * self.fy + (3 + c) * self.cy, self.cy)

    def yf(self, c, x):
        return pl.ds(c * self.fx + x, 1)

    def yc(self, c, x):
        return pl.ds(3 * self.fx + c * self.cx + x, 1)

    def yt(self, c, x):
        return pl.ds(3 * self.fx + (3 + c) * self.cx + x, 1)


def iota(shape, axis):
    return lax.broadcasted_iota(jnp.int32, shape, axis)


def below(tile, ghost):
    n = tile.shape[-1]
    return pltpu.roll(jnp.where(iota(tile.shape, 1) == 0, ghost, tile), n - 1, 1)


def above(tile, ghost):
    n = tile.shape[-1]
    return pltpu.roll(jnp.where(iota(tile.shape, 1) == n - 1, ghost, tile), 1, 1)


def above_same(tile):
    return jnp.where(iota(tile.shape, 1) == 0, tile, pltpu.roll(tile, 1, 1))


def y_minus(tile, row):
    return jnp.concatenate([row, tile[:-1]], axis=0)


def y_plus(tile, row):
    return jnp.concatenate([tile[1:], row], axis=0)


def restrict(first, second):
    total = first + second
    rows = total.shape[0] // 2
    out = jnp.zeros((rows, total.shape[1]), F32)
    where = iota(out.shape, 0)
    for j in range(rows):
        pair = total[2 * j : 2 * j + 1] + total[2 * j + 1 : 2 * j + 2]
        out = jnp.where(where == j, pair, out)
    return 0.25 * out


def columns(stretch, x, size):
    row = stretch[x : x + 1, :]
    eye = iota((size, size), 0) == iota((size, size), 1)
    return jnp.sum(jnp.where(eye, row, 0.0), axis=1, keepdims=True)


def prolong_weights(size, nz):
    y = iota((size, nz), 0)
    out = []
    for j in range(-1, size // 2 + 1):
        near = (y == 2 * j) | (y == 2 * j + 1)
        far = (y == 2 * j + 2) | (y == 2 * j - 1)
        out.append(jnp.where(near, 0.75, jnp.where(far, 0.25, 0.0)).astype(F32))
    return out


def level_force(p, lo, hi, dz, sz, dz_lo, dz_hi, mu, lam, h, hz, emit):
    count = len(p[0]) - 2
    dy, sy = {}, {}
    for c in range(3):
        for x in range(count + 2):
            own = 1 <= x <= count
            if c == 2 and not own:
                continue
            plus = y_plus(p[c][x], hi[c][x])
            minus = y_minus(p[c][x], lo[c][x])
            if c < 2:
                dy[c, x] = plus - minus
            if own:
                sy[c, x] = plus + minus
    flat = 1.0 / (4.0 * h * h)
    ih2 = 1.0 / (h * h)
    for x in range(1, count + 1):
        iz = hz(x - 1)
        iz2 = iz * iz
        slant = iz * (0.25 / h)
        dxx = [(p[c][x + 1] + p[c][x - 1] - 2.0 * p[c][x]) * ih2 for c in range(3)]
        dyy = [(sy[c, x] - 2.0 * p[c][x]) * ih2 for c in range(3)]
        dzz = [(sz[c][x - 1] - 2.0 * p[c][x]) * iz2 for c in range(3)]

        def xz(c):
            return dz[c][x + 1] - dz[c][x - 1]

        def xy(c):
            return dy[c, x + 1] - dy[c, x - 1]

        def yz(c):
            return y_plus(dz[c][x], dz_hi[c][x - 1]) - y_minus(dz[c][x], dz_lo[c][x - 1])

        grad = [
            dxx[0] + xy(1) * flat + xz(2) * slant,
            xy(0) * flat + dyy[1] + yz(2) * slant,
            (xz(0) + yz(1)) * slant + dzz[2],
        ]
        shear, both = mu(x - 1), lam(x - 1)
        emit(x - 1, [shear * (dxx[c] + dyy[c] + dzz[c]) + both * grad[c] for c in range(3)])


def forces(s, inside, nf, nc, tg, rx, ry, rd, mu_f, lam_f, iz_f, mu_c, lam_c, emit_f, emit_c):
    nz = s.nz
    pf = [[rx(0)[s.xf(c), :]] + nf[c] + [rx(1)[s.xf(c), :]] for c in range(3)]
    pc = [[rx(0)[s.xc(c), :]] + nc[c] + [rx(1)[s.xc(c), :]] for c in range(3)]
    pt = [[rx(0)[s.xt(c), :]] + tg[c] + [rx(1)[s.xt(c), :]] for c in range(3)]

    def rows(side, c, name, count, base):
        ends = [rd(xs * 2 + side)[pl.ds(base + c, 1), :] for xs in range(2)]
        return [ends[0]] + [ry(side)[name(c, x), :] for x in range(count)] + [ends[1]]

    lo_f, hi_f = ([rows(k, c, s.yf, s.fx, 0) for c in range(3)] for k in range(2))
    lo_c, hi_c = ([rows(k, c, s.yc, s.cx, 3) for c in range(3)] for k in range(2))
    zero_c = jnp.zeros((s.cy, nz), F32)
    zero_r = jnp.zeros((1, nz), F32)

    dz, sz, dz_lo, dz_hi = [], [], [], []
    for c in range(3):
        down = [below(t, zero_c) for t in pc[c]]
        up = [above(t, g) for t, g in zip(pc[c], pt[c])]
        dz.append([d - u for d, u in zip(down, up)])
        sz.append([d + u for d, u in zip(down, up)][1:-1])
        for k, (rows_c, out) in enumerate(((lo_c, dz_lo), (hi_c, dz_hi))):
            out.append(
                [
                    below(rows_c[c][x + 1], zero_r) - above(rows_c[c][x + 1], ry(k)[s.yt(c, x), :])
                    for x in range(s.cx)
                ]
                if c > 0
                else None
            )
    level_force(pc, lo_c, hi_c, dz, sz, dz_lo, dz_hi, mu_c, lam_c, 1.0, lambda x: 1.0, emit_c)

    weights = prolong_weights(s.fy, nz)
    dz, sz, dz_lo, dz_hi = [], [], [], []
    for c in range(3):

        def mixed_x(get, fx):
            i = fx // 2
            other = i - 1 if fx % 2 == 0 else i + 1
            return 0.75 * get(i + 1) + 0.25 * get(other + 1)

        dz_c, sz_c, rows_lo, rows_hi = [], [], [], []
        for fx in range(-1, s.fx + 1):
            own = 0 <= fx < s.fx
            if c == 1 and not own:
                dz_c.append(None)
                continue
            tile = mixed_x(lambda i: pc[c][i], fx)
            low = mixed_x(lambda i: lo_c[c][i], fx)
            high = mixed_x(lambda i: hi_c[c][i], fx)
            parts = [low] + [tile[j : j + 1] for j in range(s.cy)] + [high]
            ghost = sum(w * r for w, r in zip(weights, parts))
            if fx < 0:
                ghost = ghost * inside(-1, 0)
            elif not own:
                ghost = ghost * inside(1, 0)
            t = pf[c][fx + 1]
            down, up = below(t, ghost), above_same(t)
            dz_c.append(down - up)
            if own:
                sz_c.append(down + up)
                if c > 0:
                    g = (0.75 * low + 0.25 * parts[1]) * inside(0, -1)
                    r = lo_f[c][fx + 1]
                    rows_lo.append(below(r, g) - above_same(r))
                    g = (0.75 * high + 0.25 * parts[-2]) * inside(0, 1)
                    r = hi_f[c][fx + 1]
                    rows_hi.append(below(r, g) - above_same(r))
        dz.append(dz_c)
        sz.append(sz_c)
        dz_lo.append(rows_lo)
        dz_hi.append(rows_hi)
    level_force(pf, lo_f, hi_f, dz, sz, dz_lo, dz_hi, mu_f, lam_f, 0.5, iz_f, emit_f)


def top_ghost(s, nf):
    return [[restrict(nf[c][2 * i], nf[c][2 * i + 1]) for i in range(s.cx)] for c in range(3)]


def place(axes):
    gx, gy = axes
    ix, iy = lax.axis_index("gx"), lax.axis_index("gy")

    def exists(dx, dy):
        ok = None
        for here, step, count in ((ix, dx, gx), (iy, dy, gy)):
            if step:
                test = here > 0 if step < 0 else here < count - 1
                ok = test if ok is None else jnp.logical_and(ok, test)
        return ok

    def inside(dx, dy):
        return jnp.where(exists(dx, dy), 1.0, 0.0).astype(F32)

    return ix, iy, exists, inside


def relaxed(memory, omega, u):
    return memory + DT * omega * (u - memory)


def first_kernel(s, axes, *refs):
    args, refs = refs[0:17], refs[17:]
    (nf_out, nc_out, tg_out, rx_out, ry_out, rd_out), refs = refs[:6], refs[6:]
    outs, refs = {"c": refs[0:4], "f": refs[4:8]}, refs[8:]
    wide_out, refs = refs[0], refs[1:]
    held, refs = refs[0:17], refs[17:]
    levels = {"c": held[0:8], "f": held[8:16]}
    stretch_ref = held[16]
    base_f, base_c, sx, sy, sd, rx, ry, rd, load_sem, send_sem, recv_sem = refs
    ix, iy, exists, inside = place(axes)

    one = lambda test: jnp.where(test, 1, 0).astype(jnp.int32)
    along = lambda here, count: one(here > 0) + one(here < count - 1) + 1
    peers = along(ix, axes[0]) * along(iy, axes[1]) - 1
    links = []
    for k, dx in enumerate(SIDES):
        links.append(((dx, 0), sx, rx, k, 1 - k))
    for k, dy in enumerate(SIDES):
        links.append(((0, dy), sy, ry, k, 1 - k))
    for k, (dx, dy) in enumerate(CORNERS):
        links.append(((dx, dy), sd, rd, k, 3 - k))

    barrier = pltpu.get_barrier_semaphore()
    for (dx, dy), *_ in links:

        @pl.when(exists(dx, dy))
        def _():
            pl.semaphore_signal(barrier, inc=1, device_id=(ix + dx, iy + dy), device_id_type=MESH)

    loads = [pltpu.make_async_copy(a, b, load_sem.at[n]) for n, (a, b) in enumerate(zip(args, held))]
    early = [10, 14, 8, 2, 6, 0]
    late = [15, 9, 11, 12, 13, 7, 1, 3, 4, 5, 16]
    for n in early + late:
        loads[n].start()

    for (dx, dy), src, dst, k, other in links:

        @pl.when(jnp.logical_not(exists(dx, dy)))
        def _():
            for e in range(2):
                dst[e, k] = jnp.zeros(dst.shape[2:], F32)

    def net_of(level):
        u, _, memory, _, _, _, q, _ = levels[level]
        out = []
        for c in range(3):
            out.append([])
            for x in range(u.shape[1]):
                out[c].append(u[c, x] - sum(q[m, x] * memory[m, c, x] for m in range(3)))
        return out

    def pack(e, nf, nc, tg):
        for k in range(2):
            fx, cx = (0, 0) if k == 0 else (s.fx - 1, s.cx - 1)
            for c in range(3):
                sx[e, k, s.xf(c), :] = nf[c][fx]
                sx[e, k, s.xc(c), :] = nc[c][cx]
                sx[e, k, s.xt(c), :] = tg[c][cx]
            fy, cy = (0, 0) if k == 0 else (s.fy - 1, s.cy - 1)
            for c in range(3):
                for x in range(s.fx):
                    sy[e, k, s.yf(c, x), :] = nf[c][x][fy : fy + 1]
                for x in range(s.cx):
                    sy[e, k, s.yc(c, x), :] = nc[c][x][cy : cy + 1]
                    sy[e, k, s.yt(c, x), :] = tg[c][x][cy : cy + 1]
        for k, (dx, dy) in enumerate(CORNERS):
            fx, cx = (0, 0) if dx < 0 else (s.fx - 1, s.cx - 1)
            fy, cy = (0, 0) if dy < 0 else (s.fy - 1, s.cy - 1)
            for c in range(3):
                sd[e, k, pl.ds(c, 1), :] = nf[c][fx][fy : fy + 1]
                sd[e, k, pl.ds(3 + c, 1), :] = nc[c][cx][cy : cy + 1]

    def copies(e):
        for n, ((dx, dy), src, dst, k, other) in enumerate(links):
            yield (dx, dy), pltpu.make_async_remote_copy(
                src_ref=src.at[e, k],
                dst_ref=dst.at[e, other],
                send_sem=send_sem.at[e, n],
                recv_sem=recv_sem.at[e, 11 - n if n >= 4 else n ^ 1],
                device_id=(ix + dx, iy + dy),
                device_id_type=MESH,
            )

    def start(e):
        for (dx, dy), copy in reversed(list(copies(e))):

            @pl.when(exists(dx, dy))
            def _():
                copy.start()

    def sent(e):
        for (dx, dy), copy in copies(e):

            @pl.when(exists(dx, dy))
            def _():
                copy.wait_send()

    def received(e):
        for n, ((dx, dy), src, dst, k, other) in enumerate(links):

            @pl.when(exists(dx, dy))
            def _():
                pltpu.make_async_remote_copy(
                    src_ref=src.at[e, k],
                    dst_ref=dst.at[e, k],
                    send_sem=send_sem.at[e, n],
                    recv_sem=recv_sem.at[e, n],
                    device_id=(ix + dx, iy + dy),
                    device_id_type=MESH,
                ).wait_recv()

    for n in early:
        loads[n].wait()
    nf, nc = net_of("f"), net_of("c")
    tg = top_ghost(s, nf)
    pack(0, nf, nc, tg)
    pl.semaphore_wait(barrier, peers)
    start(0)

    for n in late:
        loads[n].wait()
    for level, base in (("f", base_f), ("c", base_c)):
        u, prev, memory, mu, lam, rho, q, omega = levels[level]
        new_u, new_memory, shear_out, both_out = outs[level]
        for x in range(u.shape[1]):
            scale = (DT * DT) / rho[x]
            shear_out[x] = scale * mu[x]
            both_out[x] = scale * (mu[x] + lam[x])
            for c in range(3):
                here = u[c, x]
                mem = [relaxed(memory[m, c, x], omega[m, x], here) for m in range(3)]
                kept = sum(q[m, x] * mem[m] for m in range(3))
                for m in range(3):
                    new_memory[m, c, x] = mem[m]
                new_u[c, x] = kept
                base[c, x] = 2.0 * here - prev[c, x] - kept
    for x in range(s.fx):
        wide_out[x] = jnp.broadcast_to(1.0 / columns(stretch_ref[...], x, s.fy), (s.fy, s.nz))

    received(0)

    new = {"f": [[None] * s.fx for _ in range(3)], "c": [[None] * s.cx for _ in range(3)]}

    def emit(level, base):
        def put(x, force):
            for c in range(3):
                new[level][c][x] = base[c, x] + force[c]

        return put

    at = lambda ref: (lambda x: ref[x])
    forces(
        s, inside, nf, nc, tg,
        lambda k: rx.at[0, k], lambda k: ry.at[0, k], lambda k: rd.at[0, k],
        at(outs["f"][2]), at(outs["f"][3]), at(wide_out), at(outs["c"][2]), at(outs["c"][3]),
        emit("f", base_f), emit("c", base_c),
    )
    nf, nc = new["f"], new["c"]
    tg = top_ghost(s, nf)
    pack(1, nf, nc, tg)
    start(1)
    for c in range(3):
        for x in range(s.fx):
            nf_out[c, x] = nf[c][x]
        for x in range(s.cx):
            nc_out[c, x] = nc[c][x]
            tg_out[c, x] = tg[c][x]
    for level, net in (("f", nf), ("c", nc)):
        u, _, _, _, _, _, _, omega = levels[level]
        new_u, new_memory, _, _ = outs[level]
        for x in range(u.shape[1]):
            for c in range(3):
                mid = net[c][x] + new_u[c, x]
                for m in range(3):
                    new_memory[m, c, x] = relaxed(new_memory[m, c, x], omega[m, x], mid)
                new_u[c, x] = 2.0 * mid - u[c, x]
    sent(0)
    received(1)
    for src, dst in ((rx, rx_out), (ry, ry_out), (rd, rd_out)):
        for k in range(dst.shape[0]):
            dst[k] = src[1, k]
    sent(1)


def second_kernel(s, axes, *refs):
    nf_ref, nc_ref, tg_ref, rx, ry, rd = refs[0:6]
    ins = {"c": refs[6:10], "f": refs[10:14]}
    wide = refs[14]
    uc_out, uf_out, mc_out, mf_out = refs[15:19]
    uf, uc, sem = refs[19:]
    _, _, _, inside = place(axes)
    stores = [
        pltpu.make_async_copy(src, dst, sem.at[n])
        for n, (src, dst) in enumerate(
            ((ins["f"][1], mf_out), (ins["c"][1], mc_out), (uc, uc_out), (uf, uf_out))
        )
    ]
    stores[0].start()
    stores[1].start()
    tiles = lambda ref: [[ref[c, x] for x in range(ref.shape[1])] for c in range(3)]

    def emit(level, out):
        def put(x, force):
            for c in range(3):
                out[c, x] = ins[level][0][c, x] + force[c]

        return put

    at = lambda ref: (lambda x: ref[x])
    forces(
        s, inside, tiles(nf_ref), tiles(nc_ref), tiles(tg_ref),
        lambda k: rx.at[k], lambda k: ry.at[k], lambda k: rd.at[k],
        at(ins["f"][2]), at(ins["f"][3]), at(wide), at(ins["c"][2]), at(ins["c"][3]),
        emit("f", uf), emit("c", uc),
    )
    stores[2].start()
    stores[3].start()
    for copy in stores:
        copy.wait()


def shards(axes, *args):
    s = Shape(args[8].shape, args[0].shape)
    vmem = pl.BlockSpec(memory_space=pltpu.VMEM)
    anywhere = pl.BlockSpec(memory_space=pltpu.HBM)
    held = lambda *shape: pltpu.VMEM(shape, F32)
    like = lambda a: pltpu.VMEM(a.shape, F32)
    out = lambda a: jax.ShapeDtypeStruct(a.shape, F32)
    level = lambda a: (like(a[0]), like(a[2]), like(a[3]), like(a[3]))
    mids = pl.pallas_call(
        functools.partial(first_kernel, s, axes),
        out_shape=(
            held(3, s.fx, s.fy, s.nz),
            held(3, s.cx, s.cy, s.nz),
            held(3, s.cx, s.cy, s.nz),
            held(2, s.x_rows, s.nz),
            held(2, s.y_rows, s.nz),
            held(4, s.d_rows, s.nz),
            *level(args[0:8]),
            *level(args[8:16]),
            held(s.fx, s.fy, s.nz),
        ),
        in_specs=[anywhere] * 17,
        out_specs=[vmem] * 15,
        scratch_shapes=[like(a) for a in args]
        + [held(3, s.fx, s.fy, s.nz), held(3, s.cx, s.cy, s.nz)]
        + [
            held(2, n, rows, s.nz)
            for _ in range(2)
            for n, rows in ((2, s.x_rows), (2, s.y_rows), (4, s.d_rows))
        ]
        + [
            pltpu.SemaphoreType.DMA((17,)),
            pltpu.SemaphoreType.DMA((2, 8)),
            pltpu.SemaphoreType.DMA((2, 8)),
        ],
        compiler_params=pltpu.CompilerParams(
            collective_id=0, has_side_effects=True, vmem_limit_bytes=8 * 1024 * 1024
        ),
        name="exchange",
    )(*args)
    return pl.pallas_call(
        functools.partial(second_kernel, s, axes),
        out_shape=(out(args[0]), out(args[8]), out(args[2]), out(args[10])),
        in_specs=[vmem] * 15,
        out_specs=[anywhere] * 4,
        scratch_shapes=[like(args[8]), like(args[0]), pltpu.SemaphoreType.DMA((4,))],
        compiler_params=pltpu.CompilerParams(vmem_limit_bytes=8 * 1024 * 1024),
        name="finish",
    )(*mids)


def solution(mesh):
    axes = (mesh.shape["gx"], mesh.shape["gy"])
    field = P(None, "gx", "gy", None)
    memory = P(None, None, "gx", "gy", None)
    cell = P("gx", "gy", None)
    level = (field, field, memory, cell, cell, cell, field, field)
    return jax.shard_map(
        functools.partial(shards, axes),
        mesh=mesh,
        in_specs=level + level + (P("gx", "gy"),),
        out_specs=(field, field, memory, memory),
        check_vma=False,
    )
```

```python
import functools

import jax
import jax.numpy as jnp
from jax import lax
from jax.experimental import pallas as pl
from jax.experimental.pallas import tpu as pltpu
from jax.sharding import PartitionSpec as P

STEPS = 2
DT = 0.1
MESH = pl.DeviceIdType.MESH
SIDES = (-1, 1)
CORNERS = tuple((dx, dy) for dx in SIDES for dy in SIDES)
F32 = jnp.float32


class Shape:
    def __init__(self, fine, coarse):
        _, self.fx, self.fy, self.nz = fine
        _, self.cx, self.cy, _ = coarse
        self.x_rows = 3 * self.fy + 6 * self.cy
        self.y_rows = 3 * self.fx + 6 * self.cx
        self.d_rows = 6

    def xf(self, c):
        return pl.ds(c * self.fy, self.fy)

    def xc(self, c):
        return pl.ds(3 * self.fy + c * self.cy, self.cy)

    def xt(self, c):
        return pl.ds(3 * self.fy + (3 + c) * self.cy, self.cy)

    def yf(self, c, x):
        return pl.ds(c * self.fx + x, 1)

    def yc(self, c, x):
        return pl.ds(3 * self.fx + c * self.cx + x, 1)

    def yt(self, c, x):
        return pl.ds(3 * self.fx + (3 + c) * self.cx + x, 1)


def iota(shape, axis):
    return lax.broadcasted_iota(jnp.int32, shape, axis)


def below(tile, ghost):
    n = tile.shape[-1]
    return pltpu.roll(jnp.where(iota(tile.shape, 1) == 0, ghost, tile), n - 1, 1)


def above(tile, ghost):
    n = tile.shape[-1]
    return pltpu.roll(jnp.where(iota(tile.shape, 1) == n - 1, ghost, tile), 1, 1)


def above_same(tile):
    return jnp.where(iota(tile.shape, 1) == 0, tile, pltpu.roll(tile, 1, 1))


def y_minus(tile, row):
    return jnp.concatenate([row, tile[:-1]], axis=0)


def y_plus(tile, row):
    return jnp.concatenate([tile[1:], row], axis=0)


def restrict(first, second):
    total = first + second
    rows = total.shape[0] // 2
    out = jnp.zeros((rows, total.shape[1]), F32)
    where = iota(out.shape, 0)
    for j in range(rows):
        pair = total[2 * j : 2 * j + 1] + total[2 * j + 1 : 2 * j + 2]
        out = jnp.where(where == j, pair, out)
    return 0.25 * out


def columns(stretch, x, size):
    row = stretch[x : x + 1, :]
    eye = iota((size, size), 0) == iota((size, size), 1)
    return jnp.sum(jnp.where(eye, row, 0.0), axis=1, keepdims=True)


def prolong_weights(size, nz):
    y = iota((size, nz), 0)
    out = []
    for j in range(-1, size // 2 + 1):
        near = (y == 2 * j) | (y == 2 * j + 1)
        far = (y == 2 * j + 2) | (y == 2 * j - 1)
        out.append(jnp.where(near, 0.75, jnp.where(far, 0.25, 0.0)).astype(F32))
    return out


def level_force(p, lo, hi, dz, sz, dz_lo, dz_hi, mu, lam, h, hz, emit):
    count = len(p[0]) - 2
    dy, sy = {}, {}
    for c in range(3):
        for x in range(count + 2):
            own = 1 <= x <= count
            if c == 2 and not own:
                continue
            plus = y_plus(p[c][x], hi[c][x])
            minus = y_minus(p[c][x], lo[c][x])
            if c < 2:
                dy[c, x] = plus - minus
            if own:
                sy[c, x] = plus + minus
    flat = 1.0 / (4.0 * h * h)
    ih2 = 1.0 / (h * h)
    for x in range(1, count + 1):
        iz = hz(x - 1)
        iz2 = iz * iz
        slant = iz * (0.25 / h)
        dxx = [(p[c][x + 1] + p[c][x - 1] - 2.0 * p[c][x]) * ih2 for c in range(3)]
        dyy = [(sy[c, x] - 2.0 * p[c][x]) * ih2 for c in range(3)]
        dzz = [(sz[c][x - 1] - 2.0 * p[c][x]) * iz2 for c in range(3)]

        def xz(c):
            return dz[c][x + 1] - dz[c][x - 1]

        def xy(c):
            return dy[c, x + 1] - dy[c, x - 1]

        def yz(c):
            return y_plus(dz[c][x], dz_hi[c][x - 1]) - y_minus(dz[c][x], dz_lo[c][x - 1])

        grad = [
            dxx[0] + xy(1) * flat + xz(2) * slant,
            xy(0) * flat + dyy[1] + yz(2) * slant,
            (xz(0) + yz(1)) * slant + dzz[2],
        ]
        shear, both = mu(x - 1), lam(x - 1)
        emit(x - 1, [shear * (dxx[c] + dyy[c] + dzz[c]) + both * grad[c] for c in range(3)])


def forces(s, inside, nf, nc, tg, rx, ry, rd, mu_f, lam_f, iz_f, mu_c, lam_c, emit_f, emit_c):
    nz = s.nz
    pf = [[rx(0)[s.xf(c), :]] + nf[c] + [rx(1)[s.xf(c), :]] for c in range(3)]
    pc = [[rx(0)[s.xc(c), :]] + nc[c] + [rx(1)[s.xc(c), :]] for c in range(3)]
    pt = [[rx(0)[s.xt(c), :]] + tg[c] + [rx(1)[s.xt(c), :]] for c in range(3)]

    def rows(side, c, name, count, base):
        ends = [rd(xs * 2 + side)[pl.ds(base + c, 1), :] for xs in range(2)]
        return [ends[0]] + [ry(side)[name(c, x), :] for x in range(count)] + [ends[1]]

    lo_f, hi_f = ([rows(k, c, s.yf, s.fx, 0) for c in range(3)] for k in range(2))
    lo_c, hi_c = ([rows(k, c, s.yc, s.cx, 3) for c in range(3)] for k in range(2))
    zero_c = jnp.zeros((s.cy, nz), F32)
    zero_r = jnp.zeros((1, nz), F32)

    dz, sz, dz_lo, dz_hi = [], [], [], []
    for c in range(3):
        down = [below(t, zero_c) for t in pc[c]]
        up = [above(t, g) for t, g in zip(pc[c], pt[c])]
        dz.append([d - u for d, u in zip(down, up)])
        sz.append([d + u for d, u in zip(down, up)][1:-1])
        for k, (rows_c, out) in enumerate(((lo_c, dz_lo), (hi_c, dz_hi))):
            out.append(
                [
                    below(rows_c[c][x + 1], zero_r) - above(rows_c[c][x + 1], ry(k)[s.yt(c, x), :])
                    for x in range(s.cx)
                ]
                if c > 0
                else None
            )
    level_force(pc, lo_c, hi_c, dz, sz, dz_lo, dz_hi, mu_c, lam_c, 1.0, lambda x: 1.0, emit_c)

    weights = prolong_weights(s.fy, nz)
    dz, sz, dz_lo, dz_hi = [], [], [], []
    for c in range(3):

        def mixed_x(get, fx):
            i = fx // 2
            other = i - 1 if fx % 2 == 0 else i + 1
            return 0.75 * get(i + 1) + 0.25 * get(other + 1)

        dz_c, sz_c, rows_lo, rows_hi = [], [], [], []
        for fx in range(-1, s.fx + 1):
            own = 0 <= fx < s.fx
            if c == 1 and not own:
                dz_c.append(None)
                continue
            tile = mixed_x(lambda i: pc[c][i], fx)
            low = mixed_x(lambda i: lo_c[c][i], fx)
            high = mixed_x(lambda i: hi_c[c][i], fx)
            parts = [low] + [tile[j : j + 1] for j in range(s.cy)] + [high]
            ghost = sum(w * r for w, r in zip(weights, parts))
            if fx < 0:
                ghost = ghost * inside(-1, 0)
            elif not own:
                ghost = ghost * inside(1, 0)
            t = pf[c][fx + 1]
            down, up = below(t, ghost), above_same(t)
            dz_c.append(down - up)
            if own:
                sz_c.append(down + up)
                if c > 0:
                    g = (0.75 * low + 0.25 * parts[1]) * inside(0, -1)
                    r = lo_f[c][fx + 1]
                    rows_lo.append(below(r, g) - above_same(r))
                    g = (0.75 * high + 0.25 * parts[-2]) * inside(0, 1)
                    r = hi_f[c][fx + 1]
                    rows_hi.append(below(r, g) - above_same(r))
        dz.append(dz_c)
        sz.append(sz_c)
        dz_lo.append(rows_lo)
        dz_hi.append(rows_hi)
    level_force(pf, lo_f, hi_f, dz, sz, dz_lo, dz_hi, mu_f, lam_f, 0.5, iz_f, emit_f)


def top_ghost(s, nf):
    return [[restrict(nf[c][2 * i], nf[c][2 * i + 1]) for i in range(s.cx)] for c in range(3)]


def place(axes):
    gx, gy = axes
    ix, iy = lax.axis_index("gx"), lax.axis_index("gy")

    def exists(dx, dy):
        ok = None
        for here, step, count in ((ix, dx, gx), (iy, dy, gy)):
            if step:
                test = here > 0 if step < 0 else here < count - 1
                ok = test if ok is None else jnp.logical_and(ok, test)
        return ok

    def inside(dx, dy):
        return jnp.where(exists(dx, dy), 1.0, 0.0).astype(F32)

    return ix, iy, exists, inside


def relaxed(memory, omega, u):
    return memory + DT * omega * (u - memory)


def first_kernel(s, axes, *refs):
    args, refs = refs[0:17], refs[17:]
    (nf_out, nc_out, tg_out, rx_out, ry_out, rd_out), refs = refs[:6], refs[6:]
    outs, refs = {"c": refs[0:4], "f": refs[4:8]}, refs[8:]
    wide_out, refs = refs[0], refs[1:]
    held, refs = refs[0:17], refs[17:]
    levels = {"c": held[0:8], "f": held[8:16]}
    stretch_ref = held[16]
    base_f, base_c, sx, sy, sd, rx, ry, rd, load_sem, send_sem, recv_sem = refs
    ix, iy, exists, inside = place(axes)

    one = lambda test: jnp.where(test, 1, 0).astype(jnp.int32)
    along = lambda here, count: one(here > 0) + one(here < count - 1) + 1
    peers = along(ix, axes[0]) * along(iy, axes[1]) - 1
    links = []
    for k, dx in enumerate(SIDES):
        links.append(((dx, 0), sx, rx, k, 1 - k))
    for k, dy in enumerate(SIDES):
        links.append(((0, dy), sy, ry, k, 1 - k))
    for k, (dx, dy) in enumerate(CORNERS):
        links.append(((dx, dy), sd, rd, k, 3 - k))

    barrier = pltpu.get_barrier_semaphore()
    for (dx, dy), *_ in links:

        @pl.when(exists(dx, dy))
        def _():
            pl.semaphore_signal(barrier, inc=1, device_id=(ix + dx, iy + dy), device_id_type=MESH)

    loads = [pltpu.make_async_copy(a, b, load_sem.at[n]) for n, (a, b) in enumerate(zip(args, held))]
    early = [10, 14, 8, 2, 6, 0]
    late = [15, 9, 11, 12, 13, 7, 1, 3, 4, 5, 16]
    for n in early + late:
        loads[n].start()

    for (dx, dy), src, dst, k, other in links:

        @pl.when(jnp.logical_not(exists(dx, dy)))
        def _():
            for e in range(2):
                dst[e, k] = jnp.zeros(dst.shape[2:], F32)

    def net_of(level):
        u, _, memory, _, _, _, q, _ = levels[level]
        out = []
        for c in range(3):
            out.append([])
            for x in range(u.shape[1]):
                out[c].append(u[c, x] - sum(q[m, x] * memory[m, c, x] for m in range(3)))
        return out

    def pack(e, nf, nc, tg):
        for k in range(2):
            fx, cx = (0, 0) if k == 0 else (s.fx - 1, s.cx - 1)
            for c in range(3):
                sx[e, k, s.xf(c), :] = nf[c][fx]
                sx[e, k, s.xc(c), :] = nc[c][cx]
                sx[e, k, s.xt(c), :] = tg[c][cx]
            fy, cy = (0, 0) if k == 0 else (s.fy - 1, s.cy - 1)
            for c in range(3):
                for x in range(s.fx):
                    sy[e, k, s.yf(c, x), :] = nf[c][x][fy : fy + 1]
                for x in range(s.cx):
                    sy[e, k, s.yc(c, x), :] = nc[c][x][cy : cy + 1]
                    sy[e, k, s.yt(c, x), :] = tg[c][x][cy : cy + 1]
        for k, (dx, dy) in enumerate(CORNERS):
            fx, cx = (0, 0) if dx < 0 else (s.fx - 1, s.cx - 1)
            fy, cy = (0, 0) if dy < 0 else (s.fy - 1, s.cy - 1)
            for c in range(3):
                sd[e, k, pl.ds(c, 1), :] = nf[c][fx][fy : fy + 1]
                sd[e, k, pl.ds(3 + c, 1), :] = nc[c][cx][cy : cy + 1]

    def copies(e):
        for n, ((dx, dy), src, dst, k, other) in enumerate(links):
            yield (dx, dy), pltpu.make_async_remote_copy(
                src_ref=src.at[e, k],
                dst_ref=dst.at[e, other],
                send_sem=send_sem.at[e, n],
                recv_sem=recv_sem.at[e, 11 - n if n >= 4 else n ^ 1],
                device_id=(ix + dx, iy + dy),
                device_id_type=MESH,
            )

    def start(e):
        for (dx, dy), copy in reversed(list(copies(e))):

            @pl.when(exists(dx, dy))
            def _():
                copy.start()

    def sent(e):
        for (dx, dy), copy in copies(e):

            @pl.when(exists(dx, dy))
            def _():
                copy.wait_send()

    def received(e):
        for n, ((dx, dy), src, dst, k, other) in enumerate(links):

            @pl.when(exists(dx, dy))
            def _():
                pltpu.make_async_remote_copy(
                    src_ref=src.at[e, k],
                    dst_ref=dst.at[e, k],
                    send_sem=send_sem.at[e, n],
                    recv_sem=recv_sem.at[e, n],
                    device_id=(ix + dx, iy + dy),
                    device_id_type=MESH,
                ).wait_recv()

    for n in early:
        loads[n].wait()
    nf, nc = net_of("f"), net_of("c")
    tg = top_ghost(s, nf)
    pack(0, nf, nc, tg)
    pl.semaphore_wait(barrier, peers)
    start(0)

    for n in late:
        loads[n].wait()
    for level, base in (("f", base_f), ("c", base_c)):
        u, prev, memory, mu, lam, rho, q, omega = levels[level]
        new_u, new_memory, shear_out, both_out = outs[level]
        for x in range(u.shape[1]):
            scale = (DT * DT) / rho[x]
            shear_out[x] = scale * mu[x]
            both_out[x] = scale * (mu[x] + lam[x])
            for c in range(3):
                here = u[c, x]
                mem = [relaxed(memory[m, c, x], omega[m, x], here) for m in range(3)]
                kept = sum(q[m, x] * mem[m] for m in range(3))
                for m in range(3):
                    new_memory[m, c, x] = mem[m]
                new_u[c, x] = kept
                base[c, x] = 2.0 * here - prev[c, x] - kept
    for x in range(s.fx):
        wide_out[x] = jnp.broadcast_to(1.0 / columns(stretch_ref[...], x, s.fy), (s.fy, s.nz))

    received(0)

    new = {"f": [[None] * s.fx for _ in range(3)], "c": [[None] * s.cx for _ in range(3)]}

    def emit(level, base):
        def put(x, force):
            for c in range(3):
                new[level][c][x] = base[c, x] + force[c]

        return put

    at = lambda ref: (lambda x: ref[x])
    forces(
        s, inside, nf, nc, tg,
        lambda k: rx.at[0, k], lambda k: ry.at[0, k], lambda k: rd.at[0, k],
        at(outs["f"][2]), at(outs["f"][3]), at(wide_out), at(outs["c"][2]), at(outs["c"][3]),
        emit("f", base_f), emit("c", base_c),
    )
    nf, nc = new["f"], new["c"]
    tg = top_ghost(s, nf)
    pack(1, nf, nc, tg)
    start(1)
    for c in range(3):
        for x in range(s.fx):
            nf_out[c, x] = nf[c][x]
        for x in range(s.cx):
            nc_out[c, x] = nc[c][x]
            tg_out[c, x] = tg[c][x]
    for level, net in (("f", nf), ("c", nc)):
        u, _, _, _, _, _, _, omega = levels[level]
        new_u, new_memory, _, _ = outs[level]
        for x in range(u.shape[1]):
            for c in range(3):
                mid = net[c][x] + new_u[c, x]
                for m in range(3):
                    new_memory[m, c, x] = relaxed(new_memory[m, c, x], omega[m, x], mid)
                new_u[c, x] = 2.0 * mid - u[c, x]
    sent(0)
    received(1)
    for src, dst in ((rx, rx_out), (ry, ry_out), (rd, rd_out)):
        for k in range(dst.shape[0]):
            dst[k] = src[1, k]
    sent(1)


def second_kernel(s, axes, *refs):
    nf_ref, nc_ref, tg_ref, rx, ry, rd = refs[0:6]
    ins = {"c": refs[6:10], "f": refs[10:14]}
    wide = refs[14]
    uc_out, uf_out, mc_out, mf_out = refs[15:19]
    uf, uc, sem = refs[19:]
    _, _, _, inside = place(axes)
    stores = [
        pltpu.make_async_copy(src, dst, sem.at[n])
        for n, (src, dst) in enumerate(
            ((ins["f"][1], mf_out), (ins["c"][1], mc_out), (uc, uc_out), (uf, uf_out))
        )
    ]
    stores[0].start()
    stores[1].start()
    tiles = lambda ref: [[ref[c, x] for x in range(ref.shape[1])] for c in range(3)]

    def emit(level, out):
        def put(x, force):
            for c in range(3):
                out[c, x] = ins[level][0][c, x] + force[c]

        return put

    at = lambda ref: (lambda x: ref[x])
    forces(
        s, inside, tiles(nf_ref), tiles(nc_ref), tiles(tg_ref),
        lambda k: rx.at[k], lambda k: ry.at[k], lambda k: rd.at[k],
        at(ins["f"][2]), at(ins["f"][3]), at(wide), at(ins["c"][2]), at(ins["c"][3]),
        emit("f", uf), emit("c", uc),
    )
    stores[2].start()
    stores[3].start()
    for copy in stores:
        copy.wait()


def shards(axes, *args):
    s = Shape(args[8].shape, args[0].shape)
    vmem = pl.BlockSpec(memory_space=pltpu.VMEM)
    anywhere = pl.BlockSpec(memory_space=pltpu.HBM)
    held = lambda *shape: pltpu.VMEM(shape, F32)
    like = lambda a: pltpu.VMEM(a.shape, F32)
    out = lambda a: jax.ShapeDtypeStruct(a.shape, F32)
    level = lambda a: (like(a[0]), like(a[2]), like(a[3]), like(a[3]))
    mids = pl.pallas_call(
        functools.partial(first_kernel, s, axes),
        out_shape=(
            held(3, s.fx, s.fy, s.nz),
            held(3, s.cx, s.cy, s.nz),
            held(3, s.cx, s.cy, s.nz),
            held(2, s.x_rows, s.nz),
            held(2, s.y_rows, s.nz),
            held(4, s.d_rows, s.nz),
            *level(args[0:8]),
            *level(args[8:16]),
            held(s.fx, s.fy, s.nz),
        ),
        in_specs=[anywhere] * 17,
        out_specs=[vmem] * 15,
        scratch_shapes=[like(a) for a in args]
        + [held(3, s.fx, s.fy, s.nz), held(3, s.cx, s.cy, s.nz)]
        + [
            held(2, n, rows, s.nz)
            for _ in range(2)
            for n, rows in ((2, s.x_rows), (2, s.y_rows), (4, s.d_rows))
        ]
        + [
            pltpu.SemaphoreType.DMA((17,)),
            pltpu.SemaphoreType.DMA((2, 8)),
            pltpu.SemaphoreType.DMA((2, 8)),
        ],
        compiler_params=pltpu.CompilerParams(
            collective_id=0, has_side_effects=True, vmem_limit_bytes=8 * 1024 * 1024
        ),
        name="exchange",
    )(*(pltpu.with_memory_space_constraint(a, pltpu.HBM) for a in args))
    return pl.pallas_call(
        functools.partial(second_kernel, s, axes),
        out_shape=(out(args[0]), out(args[8]), out(args[2]), out(args[10])),
        in_specs=[vmem] * 15,
        out_specs=[anywhere] * 4,
        scratch_shapes=[like(args[8]), like(args[0]), pltpu.SemaphoreType.DMA((4,))],
        compiler_params=pltpu.CompilerParams(vmem_limit_bytes=8 * 1024 * 1024),
        name="finish",
    )(*mids)


def solution(mesh):
    axes = (mesh.shape["gx"], mesh.shape["gy"])
    field = P(None, "gx", "gy", None)
    memory = P(None, None, "gx", "gy", None)
    cell = P("gx", "gy", None)
    level = (field, field, memory, cell, cell, cell, field, field)
    return jax.shard_map(
        functools.partial(shards, axes),
        mesh=mesh,
        in_specs=level + level + (P("gx", "gy"),),
        out_specs=(field, field, memory, memory),
        check_vma=False,
    )
```

```python
import functools

import jax
import jax.numpy as jnp
from jax import lax
from jax.experimental import pallas as pl
from jax.experimental.pallas import tpu as pltpu
from jax.sharding import PartitionSpec as P

STEPS = 2
DT = 0.1
MESH = pl.DeviceIdType.MESH
SIDES = (-1, 1)
CORNERS = tuple((dx, dy) for dx in SIDES for dy in SIDES)
F32 = jnp.float32


class Shape:
    def __init__(self, fine, coarse):
        _, self.fx, self.fy, self.nz = fine
        _, self.cx, self.cy, _ = coarse
        self.x_rows = 3 * self.fy + 6 * self.cy
        self.y_rows = 3 * self.fx + 6 * self.cx
        self.d_rows = 6

    def xf(self, c):
        return pl.ds(c * self.fy, self.fy)

    def xc(self, c):
        return pl.ds(3 * self.fy + c * self.cy, self.cy)

    def xt(self, c):
        return pl.ds(3 * self.fy + (3 + c) * self.cy, self.cy)

    def yf(self, c, x):
        return pl.ds(c * self.fx + x, 1)

    def yc(self, c, x):
        return pl.ds(3 * self.fx + c * self.cx + x, 1)

    def yt(self, c, x):
        return pl.ds(3 * self.fx + (3 + c) * self.cx + x, 1)


def iota(shape, axis):
    return lax.broadcasted_iota(jnp.int32, shape, axis)


def below(tile, ghost):
    n = tile.shape[-1]
    return pltpu.roll(jnp.where(iota(tile.shape, 1) == 0, ghost, tile), n - 1, 1)


def above(tile, ghost):
    n = tile.shape[-1]
    return pltpu.roll(jnp.where(iota(tile.shape, 1) == n - 1, ghost, tile), 1, 1)


def above_same(tile):
    return jnp.where(iota(tile.shape, 1) == 0, tile, pltpu.roll(tile, 1, 1))


def y_minus(tile, row):
    return jnp.concatenate([row, tile[:-1]], axis=0)


def y_plus(tile, row):
    return jnp.concatenate([tile[1:], row], axis=0)


def restrict(first, second):
    total = first + second
    rows = total.shape[0] // 2
    out = jnp.zeros((rows, total.shape[1]), F32)
    where = iota(out.shape, 0)
    for j in range(rows):
        pair = total[2 * j : 2 * j + 1] + total[2 * j + 1 : 2 * j + 2]
        out = jnp.where(where == j, pair, out)
    return 0.25 * out


def columns(stretch, x, size):
    row = stretch[x : x + 1, :]
    eye = iota((size, size), 0) == iota((size, size), 1)
    return jnp.sum(jnp.where(eye, row, 0.0), axis=1, keepdims=True)


def prolong_weights(size, nz):
    y = iota((size, nz), 0)
    out = []
    for j in range(-1, size // 2 + 1):
        near = (y == 2 * j) | (y == 2 * j + 1)
        far = (y == 2 * j + 2) | (y == 2 * j - 1)
        out.append(jnp.where(near, 0.75, jnp.where(far, 0.25, 0.0)).astype(F32))
    return out


def level_force(p, lo, hi, dz, sz, dz_lo, dz_hi, mu, lam, h, hz, emit):
    count = len(p[0]) - 2
    dy, sy = {}, {}
    for c in range(3):
        for x in range(count + 2):
            own = 1 <= x <= count
            if c == 2 and not own:
                continue
            plus = y_plus(p[c][x], hi[c][x])
            minus = y_minus(p[c][x], lo[c][x])
            if c < 2:
                dy[c, x] = plus - minus
            if own:
                sy[c, x] = plus + minus
    flat = 1.0 / (4.0 * h * h)
    ih2 = 1.0 / (h * h)
    for x in range(1, count + 1):
        iz = hz(x - 1)
        iz2 = iz * iz
        slant = iz * (0.25 / h)
        dxx = [(p[c][x + 1] + p[c][x - 1] - 2.0 * p[c][x]) * ih2 for c in range(3)]
        dyy = [(sy[c, x] - 2.0 * p[c][x]) * ih2 for c in range(3)]
        dzz = [(sz[c][x - 1] - 2.0 * p[c][x]) * iz2 for c in range(3)]

        def xz(c):
            return dz[c][x + 1] - dz[c][x - 1]

        def xy(c):
            return dy[c, x + 1] - dy[c, x - 1]

        def yz(c):
            return y_plus(dz[c][x], dz_hi[c][x - 1]) - y_minus(dz[c][x], dz_lo[c][x - 1])

        grad = [
            dxx[0] + xy(1) * flat + xz(2) * slant,
            xy(0) * flat + dyy[1] + yz(2) * slant,
            (xz(0) + yz(1)) * slant + dzz[2],
        ]
        shear, both = mu(x - 1), lam(x - 1)
        emit(x - 1, [shear * (dxx[c] + dyy[c] + dzz[c]) + both * grad[c] for c in range(3)])


def forces(s, inside, nf, nc, tg, rx, ry, rd, mu_f, lam_f, iz_f, mu_c, lam_c, emit_f, emit_c):
    nz = s.nz
    pf = [[rx(0)[s.xf(c), :]] + nf[c] + [rx(1)[s.xf(c), :]] for c in range(3)]
    pc = [[rx(0)[s.xc(c), :]] + nc[c] + [rx(1)[s.xc(c), :]] for c in range(3)]
    pt = [[rx(0)[s.xt(c), :]] + tg[c] + [rx(1)[s.xt(c), :]] for c in range(3)]

    def rows(side, c, name, count, base):
        ends = [rd(xs * 2 + side)[pl.ds(base + c, 1), :] for xs in range(2)]
        return [ends[0]] + [ry(side)[name(c, x), :] for x in range(count)] + [ends[1]]

    lo_f, hi_f = ([rows(k, c, s.yf, s.fx, 0) for c in range(3)] for k in range(2))
    lo_c, hi_c = ([rows(k, c, s.yc, s.cx, 3) for c in range(3)] for k in range(2))
    zero_c = jnp.zeros((s.cy, nz), F32)
    zero_r = jnp.zeros((1, nz), F32)

    dz, sz, dz_lo, dz_hi = [], [], [], []
    for c in range(3):
        down = [below(t, zero_c) for t in pc[c]]
        up = [above(t, g) for t, g in zip(pc[c], pt[c])]
        dz.append([d - u for d, u in zip(down, up)])
        sz.append([d + u for d, u in zip(down, up)][1:-1])
        for k, (rows_c, out) in enumerate(((lo_c, dz_lo), (hi_c, dz_hi))):
            out.append(
                [
                    below(rows_c[c][x + 1], zero_r) - above(rows_c[c][x + 1], ry(k)[s.yt(c, x), :])
                    for x in range(s.cx)
                ]
                if c > 0
                else None
            )
    level_force(pc, lo_c, hi_c, dz, sz, dz_lo, dz_hi, mu_c, lam_c, 1.0, lambda x: 1.0, emit_c)

    weights = prolong_weights(s.fy, nz)
    dz, sz, dz_lo, dz_hi = [], [], [], []
    for c in range(3):

        def mixed_x(get, fx):
            i = fx // 2
            other = i - 1 if fx % 2 == 0 else i + 1
            return 0.75 * get(i + 1) + 0.25 * get(other + 1)

        dz_c, sz_c, rows_lo, rows_hi = [], [], [], []
        for fx in range(-1, s.fx + 1):
            own = 0 <= fx < s.fx
            if c == 1 and not own:
                dz_c.append(None)
                continue
            tile = mixed_x(lambda i: pc[c][i], fx)
            low = mixed_x(lambda i: lo_c[c][i], fx)
            high = mixed_x(lambda i: hi_c[c][i], fx)
            parts = [low] + [tile[j : j + 1] for j in range(s.cy)] + [high]
            ghost = sum(w * r for w, r in zip(weights, parts))
            if fx < 0:
                ghost = ghost * inside(-1, 0)
            elif not own:
                ghost = ghost * inside(1, 0)
            t = pf[c][fx + 1]
            down, up = below(t, ghost), above_same(t)
            dz_c.append(down - up)
            if own:
                sz_c.append(down + up)
                if c > 0:
                    g = (0.75 * low + 0.25 * parts[1]) * inside(0, -1)
                    r = lo_f[c][fx + 1]
                    rows_lo.append(below(r, g) - above_same(r))
                    g = (0.75 * high + 0.25 * parts[-2]) * inside(0, 1)
                    r = hi_f[c][fx + 1]
                    rows_hi.append(below(r, g) - above_same(r))
        dz.append(dz_c)
        sz.append(sz_c)
        dz_lo.append(rows_lo)
        dz_hi.append(rows_hi)
    level_force(pf, lo_f, hi_f, dz, sz, dz_lo, dz_hi, mu_f, lam_f, 0.5, iz_f, emit_f)


def top_ghost(s, nf):
    return [[restrict(nf[c][2 * i], nf[c][2 * i + 1]) for i in range(s.cx)] for c in range(3)]


def place(axes):
    gx, gy = axes
    ix, iy = lax.axis_index("gx"), lax.axis_index("gy")

    def exists(dx, dy):
        ok = None
        for here, step, count in ((ix, dx, gx), (iy, dy, gy)):
            if step:
                test = here > 0 if step < 0 else here < count - 1
                ok = test if ok is None else jnp.logical_and(ok, test)
        return ok

    def inside(dx, dy):
        return jnp.where(exists(dx, dy), 1.0, 0.0).astype(F32)

    return ix, iy, exists, inside


def relaxed(memory, omega, u):
    return memory + DT * omega * (u - memory)


def first_kernel(s, axes, *refs):
    args, refs = refs[0:17], refs[17:]
    (nf_out, nc_out, tg_out, rx_out, ry_out, rd_out), refs = refs[:6], refs[6:]
    outs, refs = {"c": refs[0:4], "f": refs[4:8]}, refs[8:]
    wide_out, refs = refs[0], refs[1:]
    held, refs = refs[0:17], refs[17:]
    levels = {"c": held[0:8], "f": held[8:16]}
    stretch_ref = held[16]
    base_f, base_c, sx, sy, sd, rx, ry, rd, load_sem, send_sem, recv_sem = refs
    ix, iy, exists, inside = place(axes)

    one = lambda test: jnp.where(test, 1, 0).astype(jnp.int32)
    along = lambda here, count: one(here > 0) + one(here < count - 1) + 1
    peers = along(ix, axes[0]) * along(iy, axes[1]) - 1
    links = []
    for k, dx in enumerate(SIDES):
        links.append(((dx, 0), sx, rx, k, 1 - k))
    for k, dy in enumerate(SIDES):
        links.append(((0, dy), sy, ry, k, 1 - k))
    for k, (dx, dy) in enumerate(CORNERS):
        links.append(((dx, dy), sd, rd, k, 3 - k))

    barrier = pltpu.get_barrier_semaphore()
    for (dx, dy), *_ in links:

        @pl.when(exists(dx, dy))
        def _():
            pl.semaphore_signal(barrier, inc=1, device_id=(ix + dx, iy + dy), device_id_type=MESH)

    loads = [pltpu.make_async_copy(a, b, load_sem.at[n]) for n, (a, b) in enumerate(zip(args, held))]
    early = [10, 14, 8, 2, 6, 0]
    late = [15, 9, 11, 12, 13, 7, 1, 3, 4, 5, 16]
    for n in early + late:
        loads[n].start()

    for (dx, dy), src, dst, k, other in links:

        @pl.when(jnp.logical_not(exists(dx, dy)))
        def _():
            zeros = jnp.zeros(dst.shape[2:], F32)
            dst[0, k] = zeros
            for received, out in ((rx, rx_out), (ry, ry_out), (rd, rd_out)):
                if dst is received:
                    out[k] = zeros

    def net_of(level):
        u, _, memory, _, _, _, q, _ = levels[level]
        out = []
        for c in range(3):
            out.append([])
            for x in range(u.shape[1]):
                out[c].append(u[c, x] - sum(q[m, x] * memory[m, c, x] for m in range(3)))
        return out

    def pack(e, nf, nc, tg):
        for k in range(2):
            fx, cx = (0, 0) if k == 0 else (s.fx - 1, s.cx - 1)
            for c in range(3):
                sx[e, k, s.xf(c), :] = nf[c][fx]
                sx[e, k, s.xc(c), :] = nc[c][cx]
                sx[e, k, s.xt(c), :] = tg[c][cx]
            fy, cy = (0, 0) if k == 0 else (s.fy - 1, s.cy - 1)
            for c in range(3):
                for x in range(s.fx):
                    sy[e, k, s.yf(c, x), :] = nf[c][x][fy : fy + 1]
                for x in range(s.cx):
                    sy[e, k, s.yc(c, x), :] = nc[c][x][cy : cy + 1]
                    sy[e, k, s.yt(c, x), :] = tg[c][x][cy : cy + 1]
        for k, (dx, dy) in enumerate(CORNERS):
            fx, cx = (0, 0) if dx < 0 else (s.fx - 1, s.cx - 1)
            fy, cy = (0, 0) if dy < 0 else (s.fy - 1, s.cy - 1)
            for c in range(3):
                sd[e, k, pl.ds(c, 1), :] = nf[c][fx][fy : fy + 1]
                sd[e, k, pl.ds(3 + c, 1), :] = nc[c][cx][cy : cy + 1]

    def copies(e):
        for n, ((dx, dy), src, dst, k, other) in enumerate(links):
            yield (dx, dy), pltpu.make_async_remote_copy(
                src_ref=src.at[e, k],
                dst_ref=dst.at[e, other],
                send_sem=send_sem.at[e, n],
                recv_sem=recv_sem.at[e, 11 - n if n >= 4 else n ^ 1],
                device_id=(ix + dx, iy + dy),
                device_id_type=MESH,
            )

    def start(e):
        for (dx, dy), copy in reversed(list(copies(e))):

            @pl.when(exists(dx, dy))
            def _():
                copy.start()

    def finish(e):
        for (n, ((dx, dy), src, dst, k, other)), (_, copy) in zip(enumerate(links), copies(e)):

            @pl.when(exists(dx, dy))
            def _():
                pltpu.make_async_remote_copy(
                    src_ref=src.at[e, k],
                    dst_ref=dst.at[e, k],
                    send_sem=send_sem.at[e, n],
                    recv_sem=recv_sem.at[e, n],
                    device_id=(ix + dx, iy + dy),
                    device_id_type=MESH,
                ).wait_recv()
                copy.wait_send()
                if e == 1:
                    for received, out in ((rx, rx_out), (ry, ry_out), (rd, rd_out)):
                        if dst is received:
                            out[k] = dst[e, k]

    for n in early:
        loads[n].wait()
    nf, nc = net_of("f"), net_of("c")
    tg = top_ghost(s, nf)
    pack(0, nf, nc, tg)
    pl.semaphore_wait(barrier, peers)
    start(0)

    for n in late:
        loads[n].wait()
    for level, base in (("f", base_f), ("c", base_c)):
        u, prev, memory, mu, lam, rho, q, omega = levels[level]
        new_u, new_memory, shear_out, both_out = outs[level]
        for x in range(u.shape[1]):
            scale = (DT * DT) / rho[x]
            shear_out[x] = scale * mu[x]
            both_out[x] = scale * (mu[x] + lam[x])
            for c in range(3):
                here = u[c, x]
                mem = [relaxed(memory[m, c, x], omega[m, x], here) for m in range(3)]
                kept = sum(q[m, x] * mem[m] for m in range(3))
                for m in range(3):
                    new_memory[m, c, x] = mem[m]
                new_u[c, x] = kept
                base[c, x] = 2.0 * here - prev[c, x] - kept
    for x in range(s.fx):
        wide_out[x] = jnp.broadcast_to(1.0 / columns(stretch_ref[...], x, s.fy), (s.fy, s.nz))

    finish(0)

    new = {"f": [[None] * s.fx for _ in range(3)], "c": [[None] * s.cx for _ in range(3)]}

    def emit(level, base):
        def put(x, force):
            for c in range(3):
                new[level][c][x] = base[c, x] + force[c]

        return put

    at = lambda ref: (lambda x: ref[x])
    forces(
        s, inside, nf, nc, tg,
        lambda k: rx.at[0, k], lambda k: ry.at[0, k], lambda k: rd.at[0, k],
        at(outs["f"][2]), at(outs["f"][3]), at(wide_out), at(outs["c"][2]), at(outs["c"][3]),
        emit("f", base_f), emit("c", base_c),
    )
    nf, nc = new["f"], new["c"]
    tg = top_ghost(s, nf)
    pack(1, nf, nc, tg)
    start(1)
    for c in range(3):
        for x in range(s.fx):
            nf_out[c, x] = nf[c][x]
        for x in range(s.cx):
            nc_out[c, x] = nc[c][x]
            tg_out[c, x] = tg[c][x]
    for level, net in (("f", nf), ("c", nc)):
        u, _, _, _, _, _, _, omega = levels[level]
        new_u, new_memory, _, _ = outs[level]
        for x in range(u.shape[1]):
            for c in range(3):
                mid = net[c][x] + new_u[c, x]
                for m in range(3):
                    new_memory[m, c, x] = relaxed(new_memory[m, c, x], omega[m, x], mid)
                new_u[c, x] = 2.0 * mid - u[c, x]
    finish(1)


def second_kernel(s, axes, *refs):
    nf_ref, nc_ref, tg_ref, rx, ry, rd = refs[0:6]
    ins = {"c": refs[6:10], "f": refs[10:14]}
    wide = refs[14]
    uc_out, uf_out, mc_out, mf_out = refs[15:19]
    uf, uc, sem = refs[19:]
    _, _, _, inside = place(axes)
    stores = [
        pltpu.make_async_copy(src, dst, sem.at[n])
        for n, (src, dst) in enumerate(
            ((ins["f"][1], mf_out), (ins["c"][1], mc_out), (uc, uc_out), (uf, uf_out))
        )
    ]
    stores[0].start()
    stores[1].start()
    tiles = lambda ref: [[ref[c, x] for x in range(ref.shape[1])] for c in range(3)]

    def emit(level, out):
        def put(x, force):
            for c in range(3):
                out[c, x] = ins[level][0][c, x] + force[c]

        return put

    at = lambda ref: (lambda x: ref[x])
    forces(
        s, inside, tiles(nf_ref), tiles(nc_ref), tiles(tg_ref),
        lambda k: rx.at[k], lambda k: ry.at[k], lambda k: rd.at[k],
        at(ins["f"][2]), at(ins["f"][3]), at(wide), at(ins["c"][2]), at(ins["c"][3]),
        emit("f", uf), emit("c", uc),
    )
    stores[2].start()
    stores[3].start()
    for copy in stores:
        copy.wait()


def shards(axes, *args):
    s = Shape(args[8].shape, args[0].shape)
    vmem = pl.BlockSpec(memory_space=pltpu.VMEM)
    anywhere = pl.BlockSpec(memory_space=pltpu.HBM)
    held = lambda *shape: pltpu.VMEM(shape, F32)
    like = lambda a: pltpu.VMEM(a.shape, F32)
    out = lambda a: jax.ShapeDtypeStruct(a.shape, F32)
    level = lambda a: (like(a[0]), like(a[2]), like(a[3]), like(a[3]))
    mids = pl.pallas_call(
        functools.partial(first_kernel, s, axes),
        out_shape=(
            held(3, s.fx, s.fy, s.nz),
            held(3, s.cx, s.cy, s.nz),
            held(3, s.cx, s.cy, s.nz),
            held(2, s.x_rows, s.nz),
            held(2, s.y_rows, s.nz),
            held(4, s.d_rows, s.nz),
            *level(args[0:8]),
            *level(args[8:16]),
            held(s.fx, s.fy, s.nz),
        ),
        in_specs=[anywhere] * 17,
        out_specs=[vmem] * 15,
        scratch_shapes=[like(a) for a in args]
        + [held(3, s.fx, s.fy, s.nz), held(3, s.cx, s.cy, s.nz)]
        + [
            held(2, n, rows, s.nz)
            for _ in range(2)
            for n, rows in ((2, s.x_rows), (2, s.y_rows), (4, s.d_rows))
        ]
        + [
            pltpu.SemaphoreType.DMA((17,)),
            pltpu.SemaphoreType.DMA((2, 8)),
            pltpu.SemaphoreType.DMA((2, 8)),
        ],
        compiler_params=pltpu.CompilerParams(
            collective_id=0, has_side_effects=True, vmem_limit_bytes=8 * 1024 * 1024
        ),
        name="exchange",
    )(*(pltpu.with_memory_space_constraint(a, pltpu.HBM) for a in args))
    return pl.pallas_call(
        functools.partial(second_kernel, s, axes),
        out_shape=(out(args[0]), out(args[8]), out(args[2]), out(args[10])),
        in_specs=[vmem] * 15,
        out_specs=[anywhere] * 4,
        scratch_shapes=[like(args[8]), like(args[0]), pltpu.SemaphoreType.DMA((4,))],
        compiler_params=pltpu.CompilerParams(vmem_limit_bytes=8 * 1024 * 1024),
        name="finish",
    )(*mids)


def solution(mesh):
    axes = (mesh.shape["gx"], mesh.shape["gy"])
    field = P(None, "gx", "gy", None)
    memory = P(None, None, "gx", "gy", None)
    cell = P("gx", "gy", None)
    level = (field, field, memory, cell, cell, cell, field, field)
    return jax.shard_map(
        functools.partial(shards, axes),
        mesh=mesh,
        in_specs=level + level + (P("gx", "gy"),),
        out_specs=(field, field, memory, memory),
        check_vma=False,
    )
```
